512 devices in a mesh: tm: 4 (over y), prefix: 128 (over x, z, core).
Axes of the slice: x: 4, y: 4, z: 16, core: 2. Of those that a mesh axis runs over, the one named last changes fastest.
Arguments:
- traffic: bfloat16 [262144, 4096], P('prefix', 'tm'), as said below
- start_level: float32 [262144], P('prefix'), as said below
- subspace: bfloat16 [262144, 64], P('prefix'), as said below
Outputs:
- scores: float32 [64, 4096], P(None, 'tm')
- energy: float32 [4096], P('tm')
Inputs may be any that keep to these rules, and one draw needn't show every extreme that they name: `traffic`: traffic volumes of one prefix pair per bin; each series keeps one typical level across all bins. `start_level`: each series' starting level lies within a factor of two of its typical traffic. `subspace`: each column has about unit length.
All inputs are finite; a program needn't handle non-finite values.
Results may differ from the reference program's by a relative error of at most 0.003.
Values sent between devices are 32-bit elements; how exact they have to be, the bound alone decides.
No kernel may reach another device: no remote copies, remote signals or barrier semaphores. Data moves between devices by JAX's collectives and lax.ppermute only.
A program may use at most 64 MiB of HBM per device.

```python
import math
import jax
import jax.numpy as jnp
from jax import lax

K = 64
BLOCK = 256
SERIES = 262144
BINS = 4096


def shared_basis(key):
    basis_key = jax.random.fold_in(key, 5)
    basis = jnp.clip(jax.random.normal(basis_key, (SERIES, K), jnp.float32), -5.0, 5.0)
    return (basis * (1.0 / math.sqrt(SERIES))).astype(jnp.bfloat16)


def series_shape(key):
    base_key = jax.random.fold_in(key, 7)
    scale_key = jax.random.fold_in(base_key, 1)
    level_key = jax.random.fold_in(base_key, 2)
    ratio_key = jax.random.fold_in(base_key, 3)
    ranks = jnp.arange(SERIES).astype(jnp.float32)
    noise_scale = jnp.exp(jax.random.uniform(scale_key, (SERIES,), jnp.float32, math.log(0.05), math.log(0.25))) * jnp.exp(math.log(3.0) * ranks / SERIES)
    mean_level = jax.random.uniform(level_key, (SERIES,), jnp.float32, 3.0, 6.0)
    start_ratio = jax.random.uniform(ratio_key, (SERIES,), jnp.float32, 0.9, 1.1)
    return (noise_scale, mean_level, start_ratio)


def draw_subspace(key, part):
    return shared_basis(key)


def draw_traffic(key, part):
    noise_scale, mean_level, start_ratio = series_shape(key)
    basis = shared_basis(key).astype(jnp.float32)
    noise_key = jax.random.fold_in(key, 11)
    latent_key = jax.random.fold_in(key, 13)
    latent = jnp.clip(jax.random.normal(latent_key, (K, BINS), jnp.float32), -5.0, 5.0)
    fluctuation = jnp.clip(jax.random.normal(noise_key, (SERIES, BINS), jnp.float32), -5.0, 5.0)
    normal_traffic = jnp.dot(basis, latent, precision=lax.Precision.HIGHEST) * math.sqrt(SERIES / K)
    return (mean_level[:, None] + noise_scale[:, None] * fluctuation + normal_traffic).astype(jnp.bfloat16)


def draw_start_level(key, part):
    noise_scale, mean_level, start_ratio = series_shape(key)
    return (mean_level * start_ratio).astype(jnp.float32)


def setup_inputs(seed: int = 0) -> dict:
    splits = jax.random.split(jax.random.key(seed), 4)
    traffic = draw_traffic(jax.random.fold_in(splits[3], 71), 0)
    start_level = draw_start_level(jax.random.fold_in(splits[3], 71), 0)
    subspace = draw_subspace(jax.random.fold_in(splits[3], 71), 0)
    return {"traffic": traffic, "start_level": start_level, "subspace": subspace}


ewma_rate = 0.002


def reference(traffic, start_level, subspace):
    keep_rate = 1.0 - ewma_rate
    offsets = jnp.arange(BLOCK)
    weights = (ewma_rate * keep_rate ** offsets.astype(jnp.float32)).astype(jnp.bfloat16)
    distance = offsets[:, None] - offsets[None, :]
    toeplitz = jnp.where(distance >= 0, weights[jnp.clip(distance, 0, BLOCK - 1)], jnp.zeros((), jnp.bfloat16))
    powers = keep_rate ** (offsets + 1).astype(jnp.float32)
    count_blocks = BINS // BLOCK
    stacked = jnp.transpose(traffic.reshape(SERIES, count_blocks, BLOCK), (1, 0, 2))

    def advance(level_prev, block_data):
        inner_sum = jnp.dot(block_data, toeplitz.T, preferred_element_type=jnp.float32)
        level_now = inner_sum + powers[None, :] * level_prev[:, None]
        previous = jnp.concatenate([level_prev[:, None], level_now[:, :-1]], axis=1)
        residual = (block_data.astype(jnp.float32) - previous).astype(jnp.bfloat16)
        block_scores = jnp.dot(subspace.T, residual, preferred_element_type=jnp.float32)
        scores_low = block_scores.astype(jnp.bfloat16)
        normal_part = jnp.dot(subspace, scores_low, preferred_element_type=jnp.float32)
        remainder = residual.astype(jnp.float32) - normal_part
        block_energy = jnp.sum(remainder * remainder, axis=0) / SERIES
        return level_now[:, -1], (block_scores, block_energy)

    final_level, outputs = lax.scan(advance, start_level.astype(jnp.float32), stacked)
    all_scores = jnp.transpose(outputs[0], (1, 0, 2)).reshape(K, BINS)
    all_energy = outputs[1].reshape(BINS)
    return all_scores, all_energy
```

```python
import functools
import math

import jax
import jax.numpy as jnp
import ml_dtypes
import numpy as np
from jax import lax
from jax.experimental import pallas as pl
from jax.experimental.pallas import tpu as pltpu
from jax.sharding import Mesh, PartitionSpec as P

BLOCK = 256
LANES = 128
K = 64
ewma_rate = 0.002

ROWS = 256
PIECE = 72


def powers(exponents):
    return (1.0 - ewma_rate) ** np.asarray(exponents, np.float64)


def taps():
    return (ewma_rate * powers(np.arange(BLOCK))).astype(ml_dtypes.bfloat16)


def closing_kernel(x_ref, u_ref, w_ref, scale_ref, close_ref, gram_ref):
    ends = jnp.dot(x_ref[...], w_ref[...], preferred_element_type=jnp.float32)
    ends = jnp.transpose(ends * scale_ref[...])
    close = jnp.sum(ends[0:8], axis=0, keepdims=True)
    close_ref[...] = jnp.broadcast_to(close[None], close_ref.shape)

    @pl.when(pl.program_id(0) == 0)
    def _():
        gram_ref[...] = jnp.zeros_like(gram_ref)

    u = u_ref[...]
    gram_ref[...] += lax.dot_general(
        u, u, (((0,), (0,)), ((), ())), preferred_element_type=jnp.float32
    )


def main_kernel(
    shards, width,
    x_ref, u_ref, closes_ref, start_ref, gram_ref, toeplitz_ref, tail_ref, step_ref,
    out_ref, scores_ref, square_ref,
):
    place = lax.axis_index("tm")
    blocks = width // BLOCK

    @pl.when(pl.program_id(0) == 0)
    def _():
        scores_ref[...] = jnp.zeros_like(scores_ref)
        square_ref[...] = jnp.zeros_like(square_ref)

    def weight(table):
        value = jnp.float32(table[0])
        for p in range(1, shards):
            value = jnp.where(place == p, jnp.float32(table[p]), value)
        return value

    level = start_ref[...] * weight([powers(width * p) for p in range(shards)])
    for s in range(shards - 1):
        level += closes_ref[s] * weight(
            [powers(width * (p - 1 - s)) if s < p else 0.0 for p in range(shards)]
        )
    level = jnp.transpose(jnp.broadcast_to(level, (LANES, ROWS)))
    block_keep = jnp.float32(powers(BLOCK))
    u = u_ref[...]
    for b in range(blocks):
        cols = slice(b * BLOCK, (b + 1) * BLOCK)
        x = x_ref[:, cols]
        inner = jnp.dot(x, toeplitz_ref[...], preferred_element_type=jnp.float32)
        previous = inner + jnp.concatenate([level, level], axis=1) * step_ref[...]
        residual = (x.astype(jnp.float32) - previous).astype(jnp.bfloat16)
        exact = residual.astype(jnp.float32)
        square_ref[:, cols] += jnp.sum((exact * exact).reshape(ROWS // 8, 8, BLOCK), axis=0)
        scores_ref[:, cols] += lax.dot_general(
            u, residual, (((0,), (0,)), ((), ())), preferred_element_type=jnp.float32
        )
        if b + 1 < blocks:
            level = (
                jnp.dot(x, tail_ref[...], preferred_element_type=jnp.float32) + block_keep * level
            )

    @pl.when(pl.program_id(0) == pl.num_programs(0) - 1)
    def _():
        pieces = width // LANES
        per = K // pieces
        square = jnp.sum(square_ref[...], axis=0, keepdims=True)
        gram = gram_ref[...]
        empty = jnp.zeros((per // 2, LANES - K), jnp.float32)
        for j in range(pieces):
            cols = slice(j * LANES, (j + 1) * LANES)
            out_ref[j, 0:K] = scores_ref[:, cols]
            out_ref[j, K : K + 1] = square[:, cols]
            first, second = gram[j * per : j * per + per // 2], gram[j * per + per // 2 : (j + 1) * per]
            out_ref[j, K + 1 : K + 1 + per // 2] = jnp.concatenate([first, second], axis=1)
            out_ref[j, K + 1 + per // 2 :] = jnp.zeros((PIECE - K - 1 - per // 2, LANES), jnp.float32)


def energy_kernel(series, in_ref, scores_ref, energy_ref):
    pieces = in_ref.shape[0]
    half = K // pieces // 2
    rows = []
    for j in range(pieces):
        packed = in_ref[j, K + 1 : K + 1 + half]
        rows += [packed[:, :K], packed[:, K:]]
    gram = jnp.concatenate(rows, axis=0)
    high = gram.astype(jnp.bfloat16)
    rest = gram - high.astype(jnp.float32)
    middle = rest.astype(jnp.bfloat16)
    low = (rest - middle.astype(jnp.float32)).astype(jnp.bfloat16)
    for j in range(pieces):
        cols = slice(j * LANES, (j + 1) * LANES)
        scores = in_ref[j, 0:K]
        scores_ref[:, cols] = scores
        scores_low = scores.astype(jnp.bfloat16)
        spread = jnp.dot(high, scores_low, preferred_element_type=jnp.float32)
        spread += jnp.dot(middle, scores_low, preferred_element_type=jnp.float32)
        spread += jnp.dot(low, scores_low, preferred_element_type=jnp.float32)
        inside = jnp.sum(
            scores_low.astype(jnp.float32) * (2.0 * scores - spread), axis=0, keepdims=True
        )
        energy_ref[:, cols] = (in_ref[j, K : K + 1] - inside) * jnp.float32(1.0 / series)


def shards_fn(shards, total, traffic, start_level, subspace):
    series, width = traffic.shape
    blocks = width // BLOCK
    pieces = width // LANES
    tap = taps()
    closing = np.zeros((width, LANES), ml_dtypes.bfloat16)
    for b in range(blocks):
        closing[b * BLOCK : (b + 1) * BLOCK, b] = tap[::-1]
    scale = np.zeros((1, LANES), np.float32)
    scale[0, :blocks] = powers(BLOCK * (blocks - 1 - np.arange(blocks)))
    lag = np.arange(BLOCK)[None, :] - np.arange(BLOCK)[:, None] - 1
    toeplitz = np.where(lag >= 0, tap[np.maximum(lag, 0)], tap[0] * 0)
    tail = np.broadcast_to(tap[::-1, None], (BLOCK, LANES))
    step = powers(np.arange(BLOCK))[None, :].astype(np.float32)
    steps = series // ROWS

    def whole(shape):
        return pl.BlockSpec(shape, lambda i: (0,) * len(shape))

    x_spec = pl.BlockSpec((ROWS, width), lambda i: (i, 0))
    u_spec = pl.BlockSpec((ROWS, K), lambda i: (i, 0))
    line_spec = pl.BlockSpec((shards, 1, ROWS), lambda i: (0, 0, i))
    close, gram = pl.pallas_call(
        closing_kernel,
        grid=(steps,),
        in_specs=[x_spec, u_spec, whole((width, LANES)), whole((1, LANES))],
        out_specs=[line_spec, whole((K, K))],
        out_shape=[
            jax.ShapeDtypeStruct((shards, 1, series), jnp.float32),
            jax.ShapeDtypeStruct((K, K), jnp.float32),
        ],
        name="closing",
    )(traffic, subspace, jnp.asarray(closing), jnp.asarray(scale))
    closes = lax.all_to_all(close, "tm", 0, 0, tiled=True)
    part = pl.pallas_call(
        functools.partial(main_kernel, shards, width),
        grid=(steps,),
        in_specs=[
            x_spec, u_spec, line_spec, pl.BlockSpec((1, ROWS), lambda i: (0, i)), whole((K, K)),
            whole((BLOCK, BLOCK)), whole((BLOCK, LANES)), whole((1, BLOCK)),
        ],
        out_specs=whole((pieces, PIECE, LANES)),
        out_shape=jax.ShapeDtypeStruct((pieces, PIECE, LANES), jnp.float32),
        scratch_shapes=[pltpu.VMEM((K, width), jnp.float32), pltpu.VMEM((8, width), jnp.float32)],
        compiler_params=pltpu.CompilerParams(vmem_limit_bytes=32 * 1024 * 1024),
        name="residuals",
    )(
        traffic, subspace, closes, start_level.reshape(1, series), gram,
        jnp.asarray(toeplitz), jnp.asarray(tail), jnp.asarray(step),
    )
    mine = jnp.sum(lax.all_to_all(part, ("x", "core"), 0, 0, tiled=True), axis=0)
    mine = jnp.sum(lax.all_gather(mine, "z"), axis=0)
    every = lax.all_to_all(
        jnp.broadcast_to(mine[None], (pieces, PIECE, LANES)), ("x", "core"), 0, 0, tiled=True
    )
    scores, energy = pl.pallas_call(
        functools.partial(energy_kernel, total),
        out_shape=[
            jax.ShapeDtypeStruct((K, width), jnp.float32),
            jax.ShapeDtypeStruct((1, width), jnp.float32),
        ],
        name="energies",
    )(every)
    return scores, energy.reshape(width)


def solution(mesh):
    times = mesh.shape["tm"]
    fine = Mesh(mesh.devices.reshape(times, 4, 16, 2), ("tm", "x", "z", "core"))
    prefix = ("x", "z", "core")

    def program(traffic, start_level, subspace):
        return jax.shard_map(
            functools.partial(shards_fn, times, traffic.shape[0]),
            mesh=fine,
            in_specs=(P(prefix, "tm"), P(prefix), P(prefix, None)),
            out_specs=(P(None, "tm"), P("tm")),
            check_vma=False,
        )(traffic, start_level, subspace)

    return program
```

```python
import functools

import jax
import jax.numpy as jnp
import ml_dtypes
import numpy as np
from jax import lax
from jax.experimental import pallas as pl
from jax.experimental.pallas import tpu as pltpu
from jax.sharding import Mesh, PartitionSpec as P

BLOCK=256; LANES=128; K=64; ewma_rate=0.002
PIECE=40
def powers(e): return (1.0-ewma_rate)**np.asarray(e,np.float64)
def taps(): return (ewma_rate*powers(np.arange(BLOCK))).astype(ml_dtypes.bfloat16)

def closing_kernel(rows, x_hbm, tail_ref, close_ref, x_ref, sems):
    series, width = x_ref.shape
    blocks = width // BLOCK
    steps = series // rows
    copies=[pltpu.make_async_copy(x_hbm.at[pl.ds(i*rows,rows)], x_ref.at[pl.ds(i*rows,rows)], sems.at[i]) for i in range(steps)]
    for c in copies: c.start()
    tail=tail_ref[...]
    for i in range(steps):
        copies[i].wait()
        total=None
        for b in range(blocks):
            end=jnp.dot(x_ref[i*rows:(i+1)*rows, b*BLOCK:(b+1)*BLOCK], tail, preferred_element_type=jnp.float32)
            end=end*jnp.float32(powers(BLOCK*(blocks-1-b))) if b+1<blocks else end
            total=end if total is None else total+end
        line=jnp.transpose(total)[0:1]
        close_ref[:,:,i*rows:(i+1)*rows]=jnp.broadcast_to(line[None],(close_ref.shape[0],1,rows))

def main_kernel(shards, rows, unroll, x_ref, ut_ref, closes_ref, start_ref, toeplitz_ref, tail_ref, step_ref, out_ref, scores_ref, square_ref):
    series, width = x_ref.shape
    blocks = width // BLOCK
    place = lax.axis_index("tm")
    def weight(table):
        value=jnp.float32(table[0])
        for p in range(1,shards):
            value=jnp.where(place==p, jnp.float32(table[p]), value)
        return value
    w0=weight([powers(width*p) for p in range(shards)])
    ws=[weight([powers(width*(p-1-s)) if s<p else 0.0 for p in range(shards)]) for s in range(shards-1)]
    basis=ut_ref[...]
    gram=lax.dot_general(basis,basis,(((1,),(1,)),((),())),preferred_element_type=jnp.float32)
    scores_ref[...]=jnp.zeros_like(scores_ref)
    square_ref[...]=jnp.zeros_like(square_ref)
    block_keep=jnp.float32(powers(BLOCK))
    toeplitz=toeplitz_ref[...]; tail=tail_ref[...]; step=step_ref[...]
    def lap(i, carry):
        at=pl.ds(pl.multiple_of(i*rows,rows),rows)
        line=start_ref[:,at]*w0
        for s in range(shards-1):
            line+=closes_ref[s,:,at]*ws[s]
        level=jnp.transpose(jnp.broadcast_to(line,(LANES,rows)))
        ut=ut_ref[:,at]
        for b in range(blocks):
            cols=slice(b*BLOCK,(b+1)*BLOCK)
            x=x_ref[at,cols]
            inner=jnp.dot(x,toeplitz,preferred_element_type=jnp.float32)
            previous=inner+jnp.concatenate([level,level],axis=1)*step
            residual=(x.astype(jnp.float32)-previous).astype(jnp.bfloat16)
            exact=residual.astype(jnp.float32)
            square_ref[:,cols]+=jnp.sum((exact*exact).reshape(rows//8,8,BLOCK),axis=0)
            scores_ref[:,cols]+=jnp.dot(ut,residual,preferred_element_type=jnp.float32)
            if b+1<blocks:
                level=jnp.dot(x,tail,preferred_element_type=jnp.float32)+block_keep*level
        return carry
    lax.fori_loop(0,series//rows,lap,0,unroll=unroll)
    square=jnp.sum(square_ref[...],axis=0,keepdims=True)
    pieces=out_ref.shape[0]
    halves=pieces*LANES//width
    high=K//halves; per=K//pieces
    out_ref[:, high:, :]=jnp.zeros((pieces,PIECE-high,LANES),jnp.float32)
    for p in range(pieces):
        j,h=divmod(p,halves)
        cols=slice(j*LANES,(j+1)*LANES)
        out_ref[p,0:high]=scores_ref[h*high:(h+1)*high,cols]
        out_ref[p,high:high+per,0:K]=gram[p*per:(p+1)*per]
        out_ref[p,high+per:high+per+1]=square[:,cols]

def energy_kernel(series, in_ref, scores_ref, energy_ref):
    pieces=in_ref.shape[0]
    width=scores_ref.shape[1]
    halves=pieces*LANES//width
    high=K//halves; per=K//pieces
    gram=jnp.concatenate([in_ref[p,high:high+per,0:K] for p in range(pieces)],axis=0)
    top=gram.astype(jnp.bfloat16)
    rest=gram-top.astype(jnp.float32)
    middle=rest.astype(jnp.bfloat16)
    low=(rest-middle.astype(jnp.float32)).astype(jnp.bfloat16)
    for j in range(width//LANES):
        for h in range(halves):
            scores_ref[h*high:(h+1)*high,j*LANES:(j+1)*LANES]=in_ref[j*halves+h,0:high]
        energy_ref[:,j*LANES:(j+1)*LANES]=in_ref[j*halves,high+per:high+per+1]
    scores=scores_ref[...]
    scores_low=scores.astype(jnp.bfloat16)
    spread=jnp.dot(jnp.concatenate([top,middle,low],axis=0),scores_low,preferred_element_type=jnp.float32)
    spread=spread[0:K]+spread[K:2*K]+spread[2*K:]
    inside=jnp.sum(scores_low.astype(jnp.float32)*(2.0*scores-spread),axis=0,keepdims=True)
    energy_ref[...]=(energy_ref[...]-inside)*jnp.float32(1.0/series)

def consts():
    tap=taps()
    lag=np.arange(BLOCK)[None,:]-np.arange(BLOCK)[:,None]-1
    toeplitz=np.where(lag>=0,tap[np.maximum(lag,0)],tap[0]*0).astype(ml_dtypes.bfloat16)
    tail=np.broadcast_to(tap[::-1,None],(BLOCK,LANES))
    step=powers(np.arange(BLOCK))[None,:].astype(np.float32)
    return jnp.asarray(toeplitz),jnp.asarray(tail),jnp.asarray(step)

def call_closing(rows,shards,traffic,tail):
    series,width=traffic.shape
    vm=pl.BlockSpec(memory_space=pltpu.VMEM)
    return pl.pallas_call(functools.partial(closing_kernel,rows),
        in_specs=[pl.BlockSpec(memory_space=pltpu.HBM),vm],
        out_specs=[vm]*2,
        out_shape=[jax.ShapeDtypeStruct((shards,1,series),jnp.float32),pltpu.VMEM((series,width),jnp.bfloat16)],
        scratch_shapes=[pltpu.SemaphoreType.DMA((series//rows,))],
        compiler_params=pltpu.CompilerParams(vmem_limit_bytes=48*1024*1024),
        name="closing")(traffic,tail)
def call_main(rows,unroll,shards,pieces,xv,ut,closes,start,toeplitz,tail,step):
    series,width=xv.shape
    vm=pl.BlockSpec(memory_space=pltpu.VMEM)
    return pl.pallas_call(functools.partial(main_kernel,shards,rows,unroll),
        in_specs=[vm]*7,out_specs=vm,out_shape=jax.ShapeDtypeStruct((pieces,PIECE,LANES),jnp.float32),
        scratch_shapes=[pltpu.VMEM((K,width),jnp.float32),pltpu.VMEM((8,width),jnp.float32)],
        compiler_params=pltpu.CompilerParams(vmem_limit_bytes=48*1024*1024),
        name="residuals")(xv,ut,closes,start,toeplitz,tail,step)
def call_energy(total,width,every):
    vm=pl.BlockSpec(memory_space=pltpu.VMEM)
    return pl.pallas_call(functools.partial(energy_kernel,total),
        in_specs=[vm],out_specs=[vm,vm],
        out_shape=[jax.ShapeDtypeStruct((K,width),jnp.float32),jax.ShapeDtypeStruct((1,width),jnp.float32)],
        name="energies")(pltpu.with_memory_space_constraint(every,pltpu.VMEM))

ROWS_CLOSING = 512
ROWS_MAIN = 2048
GROUP = ("x", "near", "core")


def shards_fn(shards, total, traffic, start_level, subspace):
    series, width = traffic.shape
    pieces = 1
    for axis in GROUP:
        pieces *= lax.axis_size(axis)
    toeplitz, tail, step = consts()
    close, kept = call_closing(ROWS_CLOSING, shards, traffic, tail)
    closes = lax.all_to_all(close, "tm", 0, 0, tiled=True)
    part = call_main(
        ROWS_MAIN, 1, shards, pieces,
        kept, subspace.T, closes, start_level.reshape(1, series), toeplitz, tail, step,
    )
    mine = jnp.sum(lax.all_to_all(part, GROUP, 0, 0, tiled=True), axis=0)
    far = lax.axis_size("far")
    mine = jnp.sum(
        lax.all_to_all(jnp.broadcast_to(mine[None], (far,) + mine.shape), "far", 0, 0, tiled=True), axis=0
    )
    every = lax.all_to_all(
        jnp.broadcast_to(mine[None], (pieces,) + mine.shape), GROUP, 0, 0, tiled=True
    )
    scores, energy = call_energy(total, width, every)
    return scores, energy.reshape(width)


def solution(mesh):
    times = mesh.shape["tm"]
    fine = Mesh(mesh.devices.reshape(times, 4, 8, 2, 2), ("tm", "x", "far", "near", "core"))
    prefix = ("x", "far", "near", "core")

    def program(traffic, start_level, subspace):
        return jax.shard_map(
            functools.partial(shards_fn, times, traffic.shape[0]),
            mesh=fine,
            in_specs=(P(prefix, "tm"), P(prefix), P(prefix, None)),
            out_specs=(P(None, "tm"), P("tm")),
            check_vma=False,
        )(traffic, start_level, subspace)

    return program
```

```python
import functools

import jax
import jax.numpy as jnp
import ml_dtypes
import numpy as np
from jax import lax
from jax.experimental import pallas as pl
from jax.experimental.pallas import tpu as pltpu
from jax.sharding import Mesh, PartitionSpec as P

BLOCK = 256
LANES = 128
SUBLANES = 4
K = 64
ewma_rate = 0.002


def powers(exponents):
    return (1.0 - ewma_rate) ** np.asarray(exponents, np.float64)


def taps():
    return (ewma_rate * powers(np.arange(BLOCK))).astype(ml_dtypes.bfloat16)


def closing_kernel(rows, x_hbm, weights_hbm, close_ref, ends_ref, x_ref, tail_ref, sems):
    series, width = x_ref.shape
    blocks = width // BLOCK
    steps = series // rows
    ready = pltpu.make_async_copy(weights_hbm.at[:, BLOCK:], tail_ref, sems.at[steps])
    ready.start()
    copies = []
    for i in range(steps):
        at = slice(i * rows, (i + 1) * rows)
        copies.append(pltpu.make_async_copy(x_hbm.at[at], x_ref.at[at], sems.at[i]))
        copies[-1].start()
    block_keep = jnp.float32(powers(BLOCK))
    tile = (LANES, LANES)
    diagonal = lax.broadcasted_iota(jnp.int32, tile, 0) == lax.broadcasted_iota(jnp.int32, tile, 1)
    ready.wait()
    tail = tail_ref[...]
    for i in range(steps):
        at = slice(i * rows, (i + 1) * rows)
        copies[i].wait()
        level = None
        for b in range(blocks):
            end = jnp.dot(
                x_ref[at, b * BLOCK : (b + 1) * BLOCK], tail, preferred_element_type=jnp.float32
            )
            level = end if level is None else end + block_keep * level
            if b + 1 < blocks:
                ends_ref[b, at] = level
        for first in range(0, rows, LANES):
            line = jnp.sum(jnp.where(diagonal, level[first : first + LANES], 0.0), axis=0, keepdims=True)
            close_ref[:, :, i * rows + first : i * rows + first + LANES] = jnp.broadcast_to(
                line[None], (close_ref.shape[0], 1, LANES)
            )


def residual_kernel(
    shards, x_ref, ends_ref, ut_ref, closes_ref, start_ref, weights_ref, step_ref, out_ref, scores_ref
):
    series, width = x_ref.shape
    place = lax.axis_index("tm")

    def weight(table):
        value = jnp.float32(table[0])
        for p in range(1, shards):
            value = jnp.where(place == p, jnp.float32(table[p]), value)
        return value

    line = start_ref[...] * weight([powers(width * p) for p in range(shards)])
    for s in range(shards - 1):
        line += closes_ref[s] * weight(
            [powers(width * (p - 1 - s)) if s < p else 0.0 for p in range(shards)]
        )
    basis = ut_ref[...]
    gram = lax.dot_general(basis, basis, (((1,), (1,)), ((), ())), preferred_element_type=jnp.float32)
    entry = jnp.transpose(jnp.broadcast_to(line, (LANES, series)))
    step = step_ref[...]
    squares = []
    for b in range(width // BLOCK):
        cols = slice(b * BLOCK, (b + 1) * BLOCK)
        local = jnp.dot(x_ref[:, cols], weights_ref[:, :BLOCK], preferred_element_type=jnp.float32)
        level = entry if b == 0 else ends_ref[b - 1] + jnp.float32(powers(b * BLOCK)) * entry
        level = jnp.concatenate([level] * (BLOCK // LANES), axis=1)
        residual = (local - level * step).astype(jnp.bfloat16)
        exact = residual.astype(jnp.float32)
        squares.append(jnp.sum(exact * exact, axis=0, keepdims=True))
        scores_ref[:, cols] = jnp.dot(basis, residual, preferred_element_type=jnp.float32)
    square = jnp.concatenate(squares, axis=1)
    pieces, groups = out_ref.shape[:2]
    halves = pieces * LANES // width
    high = K // halves
    per = K // pieces
    for p in range(pieces):
        j, h = divmod(p, halves)
        cols = slice(j * LANES, (j + 1) * LANES)
        for q in range(groups - 1):
            first = h * high + q * SUBLANES
            out_ref[p, q] = scores_ref[first : first + SUBLANES, cols]
        mine = gram[p * per : (p + 1) * per]
        out_ref[p, groups - 1] = jnp.concatenate(
            [
                square[:, cols],
                jnp.concatenate([mine[: per // 2], mine[per // 2 :]], axis=1),
                jnp.zeros((1, LANES), jnp.float32),
            ],
            axis=0,
        )


def energy_kernel(series, in_ref, scores_ref, energy_ref):
    pieces, groups = in_ref.shape[:2]
    width = scores_ref.shape[1]
    halves = pieces * LANES // width
    high = K // halves
    per = K // pieces
    rows = []
    for p in range(pieces):
        packed = in_ref[p, groups - 1, 1 : 1 + per // 2]
        rows += [packed[:, :K], packed[:, K:]]
    gram = jnp.concatenate(rows, axis=0)
    top = gram.astype(jnp.bfloat16)
    rest = gram - top.astype(jnp.float32)
    middle = rest.astype(jnp.bfloat16)
    low = (rest - middle.astype(jnp.float32)).astype(jnp.bfloat16)
    for p in range(pieces):
        j, h = divmod(p, halves)
        cols = slice(j * LANES, (j + 1) * LANES)
        for q in range(groups - 1):
            first = h * high + q * SUBLANES
            scores_ref[first : first + SUBLANES, cols] = in_ref[p, q]
        if h == 0:
            energy_ref[:, cols] = in_ref[p, groups - 1, 0:1]
    scores = scores_ref[...]
    scores_low = scores.astype(jnp.bfloat16)
    spread = jnp.dot(
        jnp.concatenate([top, middle, low], axis=0), scores_low, preferred_element_type=jnp.float32
    )
    spread = spread[0:K] + spread[K : 2 * K] + spread[2 * K :]
    inside = jnp.sum(scores_low.astype(jnp.float32) * (2.0 * scores - spread), axis=0, keepdims=True)
    energy_ref[...] = (energy_ref[...] - inside) * jnp.float32(1.0 / series)


def constants():
    tap = taps()
    lag = np.arange(BLOCK)[None, :] - np.arange(BLOCK)[:, None] - 1
    toeplitz = np.where(lag >= 0, -tap[np.maximum(lag, 0)], tap[0] * 0).astype(tap.dtype)
    toeplitz += np.eye(BLOCK, dtype=tap.dtype)
    tail = np.broadcast_to(tap[::-1, None], (BLOCK, LANES))
    step = powers(np.arange(BLOCK))[None, :].astype(np.float32)
    return jnp.asarray(np.concatenate([toeplitz, tail], axis=1)), jnp.asarray(step)


VMEM = pl.BlockSpec(memory_space=pltpu.VMEM)
HBM = pl.BlockSpec(memory_space=pltpu.HBM)
LIMIT = pltpu.CompilerParams(vmem_limit_bytes=20 * 1024 * 1024)


def call_closing(rows, shards, traffic, weights):
    series, width = traffic.shape
    return pl.pallas_call(
        functools.partial(closing_kernel, rows),
        in_specs=[HBM, HBM],
        out_specs=[VMEM] * 3,
        out_shape=[
            jax.ShapeDtypeStruct((shards, 1, series), jnp.float32),
            pltpu.VMEM((width // BLOCK - 1, series, LANES), jnp.float32),
            pltpu.VMEM((series, width), jnp.bfloat16),
        ],
        scratch_shapes=[
            pltpu.VMEM((BLOCK, LANES), jnp.bfloat16), pltpu.SemaphoreType.DMA((series // rows + 1,))
        ],
        compiler_params=LIMIT,
        name="closing",
    )(
        pltpu.with_memory_space_constraint(traffic, pltpu.HBM),
        pltpu.with_memory_space_constraint(weights, pltpu.HBM),
    )


def call_residual(shards, pieces, kept, ends, basis, closes, start, weights, step):
    width = kept.shape[1]
    groups = K * width // (pieces * LANES * SUBLANES) + 1
    return pl.pallas_call(
        functools.partial(residual_kernel, shards),
        in_specs=[VMEM] * 7,
        out_specs=VMEM,
        out_shape=jax.ShapeDtypeStruct((pieces, groups, SUBLANES, LANES), jnp.float32),
        scratch_shapes=[pltpu.VMEM((K, width), jnp.float32)],
        compiler_params=LIMIT,
        name="residuals",
    )(kept, ends, basis, closes, start, weights, step)


def call_energy(total, width, every):
    return pl.pallas_call(
        functools.partial(energy_kernel, total),
        in_specs=[VMEM],
        out_specs=[VMEM, VMEM],
        out_shape=[
            jax.ShapeDtypeStruct((K, width), jnp.float32),
            jax.ShapeDtypeStruct((1, width), jnp.float32),
        ],
        name="energies",
    )(pltpu.with_memory_space_constraint(every, pltpu.VMEM))

ROWS = 512
GROUP = ("x", "near", "core")


def shards_fn(shards, total, traffic, start_level, subspace):
    series, width = traffic.shape
    pieces = 1
    for axis in GROUP:
        pieces *= lax.axis_size(axis)
    weights, step = constants()
    close, ends, kept = call_closing(ROWS, shards, traffic, weights)
    closes = lax.all_to_all(close, "tm", 0, 0, tiled=True)
    part = call_residual(
        shards, pieces, kept, ends, subspace.T, closes, start_level.reshape(1, series), weights, step
    )
    mine = jnp.sum(lax.all_to_all(part, GROUP, 0, 0, tiled=True), axis=0)
    far = lax.axis_size("far")
    mine = jnp.sum(
        lax.all_to_all(jnp.broadcast_to(mine[None], (far,) + mine.shape), "far", 0, 0, tiled=True), axis=0
    )
    every = lax.all_to_all(
        jnp.broadcast_to(mine[None], (pieces,) + mine.shape), GROUP, 0, 0, tiled=True
    )
    scores, energy = call_energy(total, width, every)
    return scores, energy.reshape(width)


def solution(mesh):
    times = mesh.shape["tm"]
    fine = Mesh(mesh.devices.reshape(times, 4, 8, 2, 2), ("tm", "x", "far", "near", "core"))
    prefix = ("x", "far", "near", "core")

    def program(traffic, start_level, subspace):
        return jax.shard_map(
            functools.partial(shards_fn, times, traffic.shape[0]),
            mesh=fine,
            in_specs=(P(prefix, "tm"), P(prefix), P(prefix, None)),
            out_specs=(P(None, "tm"), P("tm")),
            check_vma=False,
        )(traffic, start_level, subspace)

    return program
```

```python
import functools

import jax
import jax.numpy as jnp
import ml_dtypes
import numpy as np
from jax import lax
from jax.experimental import pallas as pl
from jax.experimental.pallas import tpu as pltpu
from jax.sharding import Mesh, PartitionSpec as P

BLOCK = 256
LANES = 128
SUBLANES = 4
K = 64
ewma_rate = 0.002


def powers(exponents):
    return (1.0 - ewma_rate) ** np.asarray(exponents, np.float64)


def taps():
    return (ewma_rate * powers(np.arange(BLOCK))).astype(ml_dtypes.bfloat16)


def closing_kernel(rows, x_hbm, weights_hbm, close_ref, ends_ref, x_ref, tail_ref, sems):
    series, width = x_ref.shape
    blocks = width // BLOCK
    steps = series // rows
    ready = pltpu.make_async_copy(weights_hbm.at[:, BLOCK:], tail_ref, sems.at[steps])
    ready.start()
    copies = []
    for i in range(steps):
        at = slice(i * rows, (i + 1) * rows)
        copies.append(pltpu.make_async_copy(x_hbm.at[at], x_ref.at[at], sems.at[i]))
        copies[-1].start()
    block_keep = jnp.float32(powers(BLOCK))
    tile = (LANES, LANES)
    diagonal = lax.broadcasted_iota(jnp.int32, tile, 0) == lax.broadcasted_iota(jnp.int32, tile, 1)
    ready.wait()
    tail = tail_ref[...]
    for i in range(steps):
        at = slice(i * rows, (i + 1) * rows)
        copies[i].wait()
        level = None
        for b in range(blocks):
            end = jnp.dot(
                x_ref[at, b * BLOCK : (b + 1) * BLOCK], tail, preferred_element_type=jnp.float32
            )
            level = end if level is None else end + block_keep * level
            if b + 1 < blocks:
                ends_ref[b, at] = level
        for first in range(0, rows, LANES):
            line = jnp.sum(jnp.where(diagonal, level[first : first + LANES], 0.0), axis=0, keepdims=True)
            close_ref[:, :, i * rows + first : i * rows + first + LANES] = jnp.broadcast_to(
                line[None], (close_ref.shape[0], 1, LANES)
            )


def residual_kernel(
    shards, x_ref, ends_ref, ut_ref, closes_ref, start_ref, weights_ref, step_ref, out_ref, scores_ref
):
    series, width = x_ref.shape
    place = lax.axis_index("tm")

    def weight(table):
        value = jnp.float32(table[0])
        for p in range(1, shards):
            value = jnp.where(place == p, jnp.float32(table[p]), value)
        return value

    line = start_ref[...] * weight([powers(width * p) for p in range(shards)])
    for s in range(shards - 1):
        line += closes_ref[s] * weight(
            [powers(width * (p - 1 - s)) if s < p else 0.0 for p in range(shards)]
        )
    basis = ut_ref[...]
    gram = lax.dot_general(basis, basis, (((1,), (1,)), ((), ())), preferred_element_type=jnp.float32)
    entry = jnp.transpose(jnp.broadcast_to(line, (LANES, series)))
    step = step_ref[...]
    squares = []
    for b in range(width // BLOCK):
        cols = slice(b * BLOCK, (b + 1) * BLOCK)
        local = jnp.dot(x_ref[:, cols], weights_ref[:, :BLOCK], preferred_element_type=jnp.float32)
        level = entry if b == 0 else ends_ref[b - 1] + jnp.float32(powers(b * BLOCK)) * entry
        level = jnp.concatenate([level] * (BLOCK // LANES), axis=1)
        residual = (local - level * step).astype(jnp.bfloat16)
        exact = residual.astype(jnp.float32)
        squares.append(jnp.sum(exact * exact, axis=0, keepdims=True))
        scores_ref[:, cols] = jnp.dot(basis, residual, preferred_element_type=jnp.float32)
    square = jnp.concatenate(squares, axis=1)
    pieces, groups = out_ref.shape[:2]
    halves = pieces * LANES // width
    high = K // halves
    per = K // pieces
    for p in range(pieces):
        j, h = divmod(p, halves)
        cols = slice(j * LANES, (j + 1) * LANES)
        for q in range(groups - 1):
            first = h * high + q * SUBLANES
            out_ref[p, q] = scores_ref[first : first + SUBLANES, cols]
        mine = gram[p * per : (p + 1) * per]
        out_ref[p, groups - 1] = jnp.concatenate(
            [
                square[:, cols],
                jnp.concatenate([mine[: per // 2], mine[per // 2 :]], axis=1),
                jnp.zeros((1, LANES), jnp.float32),
            ],
            axis=0,
        )


def energy_kernel(series, in_ref, scores_ref, energy_ref):
    pieces, groups = in_ref.shape[:2]
    width = scores_ref.shape[1]
    halves = pieces * LANES // width
    high = K // halves
    per = K // pieces
    rows = []
    for p in range(pieces):
        packed = in_ref[p, groups - 1, 1 : 1 + per // 2]
        rows += [packed[:, :K], packed[:, K:]]
    gram = jnp.concatenate(rows, axis=0)
    top = gram.astype(jnp.bfloat16)
    rest = gram - top.astype(jnp.float32)
    middle = rest.astype(jnp.bfloat16)
    low = (rest - middle.astype(jnp.float32)).astype(jnp.bfloat16)
    for p in range(pieces):
        j, h = divmod(p, halves)
        cols = slice(j * LANES, (j + 1) * LANES)
        for q in range(groups - 1):
            first = h * high + q * SUBLANES
            scores_ref[first : first + SUBLANES, cols] = in_ref[p, q]
        if h == 0:
            energy_ref[:, cols] = in_ref[p, groups - 1, 0:1]
    scores = scores_ref[...]
    scores_low = scores.astype(jnp.bfloat16)
    spread = jnp.dot(
        jnp.concatenate([top, middle, low], axis=0), scores_low, preferred_element_type=jnp.float32
    )
    spread = spread[0:K] + spread[K : 2 * K] + spread[2 * K :]
    inside = jnp.sum(scores_low.astype(jnp.float32) * (2.0 * scores - spread), axis=0, keepdims=True)
    energy_ref[...] = (energy_ref[...] - inside) * jnp.float32(1.0 / series)


def constants():
    tap = taps()
    lag = np.arange(BLOCK)[None, :] - np.arange(BLOCK)[:, None] - 1
    toeplitz = np.where(lag >= 0, -tap[np.maximum(lag, 0)], tap[0] * 0).astype(tap.dtype)
    toeplitz += np.eye(BLOCK, dtype=tap.dtype)
    tail = np.broadcast_to(tap[::-1, None], (BLOCK, LANES))
    step = powers(np.arange(BLOCK))[None, :].astype(np.float32)
    return jnp.asarray(np.concatenate([toeplitz, tail], axis=1)), jnp.asarray(step)


VMEM = pl.BlockSpec(memory_space=pltpu.VMEM)
HBM = pl.BlockSpec(memory_space=pltpu.HBM)
LIMIT = pltpu.CompilerParams(vmem_limit_bytes=20 * 1024 * 1024)


def call_closing(rows, shards, traffic, weights):
    series, width = traffic.shape
    return pl.pallas_call(
        functools.partial(closing_kernel, rows),
        in_specs=[HBM, HBM],
        out_specs=[VMEM] * 3,
        out_shape=[
            jax.ShapeDtypeStruct((shards, 1, series), jnp.float32),
            pltpu.VMEM((width // BLOCK - 1, series, LANES), jnp.float32),
            pltpu.VMEM((series, width), jnp.bfloat16),
        ],
        scratch_shapes=[
            pltpu.VMEM((BLOCK, LANES), jnp.bfloat16), pltpu.SemaphoreType.DMA((series // rows + 1,))
        ],
        compiler_params=LIMIT,
        name="closing",
    )(
        pltpu.with_memory_space_constraint(traffic, pltpu.HBM),
        pltpu.with_memory_space_constraint(weights, pltpu.HBM),
    )


def call_residual(shards, pieces, kept, ends, basis, closes, start, weights, step):
    width = kept.shape[1]
    groups = K * width // (pieces * LANES * SUBLANES) + 1
    return pl.pallas_call(
        functools.partial(residual_kernel, shards),
        in_specs=[VMEM] * 7,
        out_specs=VMEM,
        out_shape=jax.ShapeDtypeStruct((pieces, groups, SUBLANES, LANES), jnp.float32),
        scratch_shapes=[pltpu.VMEM((K, width), jnp.float32)],
        compiler_params=LIMIT,
        name="residuals",
    )(kept, ends, basis, closes, start, weights, step)


def call_energy(total, width, every):
    return pl.pallas_call(
        functools.partial(energy_kernel, total),
        in_specs=[VMEM],
        out_specs=[VMEM, VMEM],
        out_shape=[
            jax.ShapeDtypeStruct((K, width), jnp.float32),
            jax.ShapeDtypeStruct((1, width), jnp.float32),
        ],
        name="energies",
    )(pltpu.with_memory_space_constraint(every, pltpu.VMEM))

ROWS = 512
GROUP = ("x", "near", "core")

NEAR_FIRST = 11
FAR_FIRST = 5


def order(size, first):
    return [[(first + i) % size for i in range(size)]]


def exchange(x, axes, groups):
    return lax.all_to_all(x, axes, 0, 0, axis_index_groups=groups, tiled=True)


def shards_fn(shards, total, traffic, start_level, subspace):
    series, width = traffic.shape
    pieces = 1
    for axis in GROUP:
        pieces *= lax.axis_size(axis)
    weights, step = constants()
    close, ends, kept = call_closing(ROWS, shards, traffic, weights)
    closes = lax.all_to_all(close, "tm", 0, 0, tiled=True)
    part = call_residual(
        shards, pieces, kept, ends, subspace.T, closes, start_level.reshape(1, series), weights, step
    )
    near = order(pieces, NEAR_FIRST)
    far = lax.axis_size("far")
    mine = jnp.sum(exchange(part, GROUP, near), axis=0)
    mine = jnp.sum(
        exchange(jnp.broadcast_to(mine[None], (far,) + mine.shape), "far", order(far, FAR_FIRST)), axis=0
    )
    every = exchange(jnp.broadcast_to(mine[None], (pieces,) + mine.shape), GROUP, near)
    scores, energy = call_energy(total, width, every)
    return scores, energy.reshape(width)


def solution(mesh):
    times = mesh.shape["tm"]
    fine = Mesh(mesh.devices.reshape(times, 4, 8, 2, 2), ("tm", "x", "far", "near", "core"))
    prefix = ("x", "far", "near", "core")

    def program(traffic, start_level, subspace):
        return jax.shard_map(
            functools.partial(shards_fn, times, traffic.shape[0]),
            mesh=fine,
            in_specs=(P(prefix, "tm"), P(prefix), P(prefix, None)),
            out_specs=(P(None, "tm"), P("tm")),
            check_vma=False,
        )(traffic, start_level, subspace)

    return program
```

```python
import functools

import jax
import jax.numpy as jnp
import ml_dtypes
import numpy as np
from jax import lax
from jax.experimental import pallas as pl
from jax.experimental.pallas import tpu as pltpu
from jax.sharding import PartitionSpec as P

BLOCK = 256
LANES = 128
SUBLANES = 4
K = 64
ewma_rate = 0.002


def powers(exponents):
    return (1.0 - ewma_rate) ** np.asarray(exponents, np.float64)


def taps():
    return (ewma_rate * powers(np.arange(BLOCK))).astype(ml_dtypes.bfloat16)


def closing_kernel(rows, x_hbm, weights_hbm, close_ref, ends_ref, x_ref, tail_ref, sems):
    series, width = x_ref.shape
    blocks = width // BLOCK
    steps = series // rows
    ready = pltpu.make_async_copy(weights_hbm.at[:, BLOCK:], tail_ref, sems.at[steps])
    ready.start()
    copies = []
    for i in range(steps):
        at = slice(i * rows, (i + 1) * rows)
        copies.append(pltpu.make_async_copy(x_hbm.at[at], x_ref.at[at], sems.at[i]))
        copies[-1].start()
    block_keep = jnp.float32(powers(BLOCK))
    tile = (LANES, LANES)
    diagonal = lax.broadcasted_iota(jnp.int32, tile, 0) == lax.broadcasted_iota(jnp.int32, tile, 1)
    ready.wait()
    tail = tail_ref[...]
    for i in range(steps):
        at = slice(i * rows, (i + 1) * rows)
        copies[i].wait()
        level = None
        for b in range(blocks):
            end = jnp.dot(
                x_ref[at, b * BLOCK : (b + 1) * BLOCK], tail, preferred_element_type=jnp.float32
            )
            level = end if level is None else end + block_keep * level
            if b + 1 < blocks:
                ends_ref[b, at] = level
        for first in range(0, rows, LANES):
            line = jnp.sum(jnp.where(diagonal, level[first : first + LANES], 0.0), axis=0, keepdims=True)
            close_ref[:, :, i * rows + first : i * rows + first + LANES] = jnp.broadcast_to(
                line[None], (close_ref.shape[0], 1, LANES)
            )


def residual_kernel(
    shards, x_ref, ends_ref, ut_ref, closes_ref, start_ref, weights_ref, step_ref, out_ref, scores_ref
):
    series, width = x_ref.shape
    place = lax.axis_index("tm")

    def weight(table):
        value = jnp.float32(table[0])
        for p in range(1, shards):
            value = jnp.where(place == p, jnp.float32(table[p]), value)
        return value

    line = start_ref[...] * weight([powers(width * p) for p in range(shards)])
    for s in range(shards - 1):
        line += closes_ref[(s - TIME_FIRST) % shards] * weight(
            [powers(width * (p - 1 - s)) if s < p else 0.0 for p in range(shards)]
        )
    basis = ut_ref[...]
    gram = lax.dot_general(basis, basis, (((1,), (1,)), ((), ())), preferred_element_type=jnp.float32)
    entry = jnp.transpose(jnp.broadcast_to(line, (LANES, series)))
    step = step_ref[...]
    squares = []
    for b in range(width // BLOCK):
        cols = slice(b * BLOCK, (b + 1) * BLOCK)
        local = jnp.dot(x_ref[:, cols], weights_ref[:, :BLOCK], preferred_element_type=jnp.float32)
        level = entry if b == 0 else ends_ref[b - 1] + jnp.float32(powers(b * BLOCK)) * entry
        level = jnp.concatenate([level] * (BLOCK // LANES), axis=1)
        residual = (local - level * step).astype(jnp.bfloat16)
        exact = residual.astype(jnp.float32)
        squares.append(jnp.sum(exact * exact, axis=0, keepdims=True))
        scores_ref[:, cols] = jnp.dot(basis, residual, preferred_element_type=jnp.float32)
    square = jnp.concatenate(squares, axis=1)
    pieces, groups = out_ref.shape[:2]
    halves = pieces * LANES // width
    high = K // halves
    per = K // pieces
    for p in range(pieces):
        j, h = divmod(p, halves)
        cols = slice(j * LANES, (j + 1) * LANES)
        for q in range(groups - 1):
            first = h * high + q * SUBLANES
            out_ref[p, q] = scores_ref[first : first + SUBLANES, cols]
        mine = gram[p * per : (p + 1) * per]
        out_ref[p, groups - 1] = jnp.concatenate(
            [
                square[:, cols],
                jnp.concatenate([mine[: per // 2], mine[per // 2 :]], axis=1),
                jnp.zeros((1, LANES), jnp.float32),
            ],
            axis=0,
        )


def energy_kernel(series, in_ref, scores_ref, energy_ref):
    pieces, groups = in_ref.shape[:2]
    width = scores_ref.shape[1]
    halves = pieces * LANES // width
    high = K // halves
    per = K // pieces
    rows = []
    for p in range(pieces):
        packed = in_ref[p, groups - 1, 1 : 1 + per // 2]
        rows += [packed[:, :K], packed[:, K:]]
    gram = jnp.concatenate(rows, axis=0)
    top = gram.astype(jnp.bfloat16)
    rest = gram - top.astype(jnp.float32)
    middle = rest.astype(jnp.bfloat16)
    low = (rest - middle.astype(jnp.float32)).astype(jnp.bfloat16)
    for p in range(pieces):
        j, h = divmod(p, halves)
        cols = slice(j * LANES, (j + 1) * LANES)
        for q in range(groups - 1):
            first = h * high + q * SUBLANES
            scores_ref[first : first + SUBLANES, cols] = in_ref[p, q]
        if h == 0:
            energy_ref[:, cols] = in_ref[p, groups - 1, 0:1]
    scores = scores_ref[...]
    scores_low = scores.astype(jnp.bfloat16)
    spread = jnp.dot(
        jnp.concatenate([top, middle, low], axis=0), scores_low, preferred_element_type=jnp.float32
    )
    spread = spread[0:K] + spread[K : 2 * K] + spread[2 * K :]
    inside = jnp.sum(scores_low.astype(jnp.float32) * (2.0 * scores - spread), axis=0, keepdims=True)
    energy_ref[...] = (energy_ref[...] - inside) * jnp.float32(1.0 / series)


def constants():
    tap = taps()
    lag = np.arange(BLOCK)[None, :] - np.arange(BLOCK)[:, None] - 1
    toeplitz = np.where(lag >= 0, -tap[np.maximum(lag, 0)], tap[0] * 0).astype(tap.dtype)
    toeplitz += np.eye(BLOCK, dtype=tap.dtype)
    tail = np.broadcast_to(tap[::-1, None], (BLOCK, LANES))
    step = powers(np.arange(BLOCK))[None, :].astype(np.float32)
    return jnp.asarray(np.concatenate([toeplitz, tail], axis=1)), jnp.asarray(step)


VMEM = pl.BlockSpec(memory_space=pltpu.VMEM)
HBM = pl.BlockSpec(memory_space=pltpu.HBM)
LIMIT = pltpu.CompilerParams(vmem_limit_bytes=20 * 1024 * 1024)


def call_closing(rows, shards, traffic, weights):
    series, width = traffic.shape
    return pl.pallas_call(
        functools.partial(closing_kernel, rows),
        in_specs=[HBM, HBM],
        out_specs=[VMEM] * 3,
        out_shape=[
            jax.ShapeDtypeStruct((shards, 1, series), jnp.float32),
            pltpu.VMEM((width // BLOCK - 1, series, LANES), jnp.float32),
            pltpu.VMEM((series, width), jnp.bfloat16),
        ],
        scratch_shapes=[
            pltpu.VMEM((BLOCK, LANES), jnp.bfloat16), pltpu.SemaphoreType.DMA((series // rows + 1,))
        ],
        compiler_params=LIMIT,
        name="closing",
    )(
        pltpu.with_memory_space_constraint(traffic, pltpu.HBM),
        pltpu.with_memory_space_constraint(weights, pltpu.HBM),
    )


def call_residual(shards, pieces, kept, ends, basis, closes, start, weights, step):
    width = kept.shape[1]
    groups = K * width // (pieces * LANES * SUBLANES) + 1
    return pl.pallas_call(
        functools.partial(residual_kernel, shards),
        in_specs=[VMEM] * 7,
        out_specs=VMEM,
        out_shape=jax.ShapeDtypeStruct((pieces, groups, SUBLANES, LANES), jnp.float32),
        scratch_shapes=[pltpu.VMEM((K, width), jnp.float32)],
        compiler_params=LIMIT,
        name="residuals",
    )(kept, ends, basis, closes, start, weights, step)


def call_energy(total, width, every):
    return pl.pallas_call(
        functools.partial(energy_kernel, total),
        in_specs=[VMEM],
        out_specs=[VMEM, VMEM],
        out_shape=[
            jax.ShapeDtypeStruct((K, width), jnp.float32),
            jax.ShapeDtypeStruct((1, width), jnp.float32),
        ],
        name="energies",
    )(pltpu.with_memory_space_constraint(every, pltpu.VMEM))

ROWS = 512

NEAR_FIRST = 11
FAR_FIRST = 5
TIME_FIRST = 2


def rotated(items, first):
    items = list(items)
    return items[first:] + items[:first]


def stages(x_size, z_size, cores):
    pairs = z_size // 2

    def device(x, pair, which, core):
        z = 2 * pair + (which if pair < pairs // 2 else 1 - which)
        return (x * z_size + z) * cores + core

    places = [(x, which, core) for x in range(x_size) for which in range(2) for core in range(cores)]
    near = [
        [device(x, pair, which, core) for x, which, core in rotated(places, NEAR_FIRST)]
        for pair in range(pairs)
    ]
    far = [
        [device(x, pair, which, core) for pair in rotated(range(pairs), FAR_FIRST)]
        for x, which, core in places
    ]
    return near, far


def exchange(x, axis, groups):
    return lax.all_to_all(x, axis, 0, 0, axis_index_groups=groups, tiled=True)


def shards_fn(shards, total, traffic, start_level, subspace):
    series, width = traffic.shape
    near, far = stages(4, 16, 2)
    pieces = len(near[0])
    weights, step = constants()
    close, ends, kept = call_closing(ROWS, shards, traffic, weights)
    closes = exchange(close, "tm", [rotated(range(shards), TIME_FIRST)])
    part = call_residual(
        shards, pieces, kept, ends, subspace.T, closes, start_level.reshape(1, series), weights, step
    )
    mine = jnp.sum(exchange(part, "prefix", near), axis=0)
    mine = jnp.broadcast_to(mine[None], (len(far[0]),) + mine.shape)
    mine = jnp.sum(exchange(mine, "prefix", far), axis=0)
    every = exchange(jnp.broadcast_to(mine[None], (pieces,) + mine.shape), "prefix", near)
    scores, energy = call_energy(total, width, every)
    return scores, energy.reshape(width)


def solution(mesh):
    def program(traffic, start_level, subspace):
        return jax.shard_map(
            functools.partial(shards_fn, mesh.shape["tm"], traffic.shape[0]),
            mesh=mesh,
            in_specs=(P("prefix", "tm"), P("prefix"), P("prefix", None)),
            out_specs=(P(None, "tm"), P("tm")),
            check_vma=False,
        )(traffic, start_level, subspace)

    return program
```

```python
import functools

import jax
import jax.numpy as jnp
import ml_dtypes
import numpy as np
from jax import lax
from jax.experimental import pallas as pl
from jax.experimental.pallas import tpu as pltpu
from jax.sharding import PartitionSpec as P

BLOCK = 256
LANES = 128
SUBLANES = 4
K = 64
ewma_rate = 0.002


def powers(exponents):
    return (1.0 - ewma_rate) ** np.asarray(exponents, np.float64)


def taps():
    return (ewma_rate * powers(np.arange(BLOCK))).astype(ml_dtypes.bfloat16)


def closing_kernel(rows, x_hbm, weights_hbm, close_ref, ends_ref, x_ref, tail_ref, sems):
    series, width = x_ref.shape
    blocks = width // BLOCK
    steps = series // rows
    ready = pltpu.make_async_copy(weights_hbm.at[:, BLOCK:], tail_ref, sems.at[steps])
    ready.start()
    copies = []
    for i in range(steps):
        at = slice(i * rows, (i + 1) * rows)
        copies.append(pltpu.make_async_copy(x_hbm.at[at], x_ref.at[at], sems.at[i]))
        copies[-1].start()
    block_keep = jnp.float32(powers(BLOCK))
    tile = (LANES, LANES)
    diagonal = lax.broadcasted_iota(jnp.int32, tile, 0) == lax.broadcasted_iota(jnp.int32, tile, 1)
    ready.wait()
    tail = tail_ref[...]
    for i in range(steps):
        at = slice(i * rows, (i + 1) * rows)
        copies[i].wait()
        level = None
        for b in range(blocks):
            end = jnp.dot(
                x_ref[at, b * BLOCK : (b + 1) * BLOCK], tail, preferred_element_type=jnp.float32
            )
            level = end if level is None else end + block_keep * level
            if b + 1 < blocks:
                ends_ref[b, at] = level
        for first in range(0, rows, LANES):
            line = jnp.sum(jnp.where(diagonal, level[first : first + LANES], 0.0), axis=0, keepdims=True)
            close_ref[:, :, i * rows + first : i * rows + first + LANES] = jnp.broadcast_to(
                line[None], (close_ref.shape[0], 1, LANES)
            )


def residual_kernel(
    shards, x_ref, ends_ref, ut_ref, closes_ref, start_ref, weights_ref, step_ref, out_ref, scores_ref
):
    series, width = x_ref.shape
    place = lax.axis_index("tm")

    def weight(table):
        value = jnp.float32(table[0])
        for p in range(1, shards):
            value = jnp.where(place == p, jnp.float32(table[p]), value)
        return value

    line = start_ref[...] * weight([powers(width * p) for p in range(shards)])
    for s in range(shards - 1):
        line += closes_ref[(s - TIME_FIRST) % shards] * weight(
            [powers(width * (p - 1 - s)) if s < p else 0.0 for p in range(shards)]
        )
    basis = ut_ref[...]
    gram = lax.dot_general(basis, basis, (((1,), (1,)), ((), ())), preferred_element_type=jnp.float32)
    entry = jnp.transpose(jnp.broadcast_to(line, (LANES, series)))
    step = step_ref[...]
    squares = []
    residuals = []
    for b in range(width // BLOCK):
        cols = slice(b * BLOCK, (b + 1) * BLOCK)
        local = jnp.dot(x_ref[:, cols], weights_ref[:, :BLOCK], preferred_element_type=jnp.float32)
        level = entry if b == 0 else ends_ref[b - 1] + jnp.float32(powers(b * BLOCK)) * entry
        level = jnp.concatenate([level] * (BLOCK // LANES), axis=1)
        residual = (local - level * step).astype(jnp.bfloat16)
        exact = residual.astype(jnp.float32)
        squares.append(jnp.sum(exact * exact, axis=0, keepdims=True))
        residuals.append(residual)
    for b in range(width // BLOCK):
        scores_ref[:, b * BLOCK : (b + 1) * BLOCK] = jnp.dot(
            basis, residuals[b], preferred_element_type=jnp.float32
        )
    square = jnp.concatenate(squares, axis=1)
    pieces, groups = out_ref.shape[:2]
    halves = pieces * LANES // width
    high = K // halves
    per = K // pieces
    for p in range(pieces):
        j, h = divmod(p, halves)
        cols = slice(j * LANES, (j + 1) * LANES)
        for q in range(groups - 1):
            first = h * high + q * SUBLANES
            out_ref[p, q] = scores_ref[first : first + SUBLANES, cols]
        mine = gram[p * per : (p + 1) * per]
        out_ref[p, groups - 1] = jnp.concatenate(
            [
                square[:, cols],
                jnp.concatenate([mine[: per // 2], mine[per // 2 :]], axis=1),
                jnp.zeros((1, LANES), jnp.float32),
            ],
            axis=0,
        )


def energy_kernel(series, in_ref, scores_ref, energy_ref):
    pieces, groups = in_ref.shape[:2]
    width = scores_ref.shape[1]
    halves = pieces * LANES // width
    high = K // halves
    per = K // pieces
    rows = []
    for p in range(pieces):
        packed = in_ref[p, groups - 1, 1 : 1 + per // 2]
        rows += [packed[:, :K], packed[:, K:]]
    gram = jnp.concatenate(rows, axis=0)
    top = gram.astype(jnp.bfloat16)
    rest = gram - top.astype(jnp.float32)
    middle = rest.astype(jnp.bfloat16)
    low = (rest - middle.astype(jnp.float32)).astype(jnp.bfloat16)
    for p in range(pieces):
        j, h = divmod(p, halves)
        cols = slice(j * LANES, (j + 1) * LANES)
        for q in range(groups - 1):
            first = h * high + q * SUBLANES
            scores_ref[first : first + SUBLANES, cols] = in_ref[p, q]
        if h == 0:
            energy_ref[:, cols] = in_ref[p, groups - 1, 0:1]
    scores = scores_ref[...]
    scores_low = scores.astype(jnp.bfloat16)
    spread = jnp.dot(
        jnp.concatenate([top, middle, low], axis=0), scores_low, preferred_element_type=jnp.float32
    )
    spread = spread[0:K] + spread[K : 2 * K] + spread[2 * K :]
    inside = jnp.sum(scores_low.astype(jnp.float32) * (2.0 * scores - spread), axis=0, keepdims=True)
    energy_ref[...] = (energy_ref[...] - inside) * jnp.float32(1.0 / series)


def constants():
    tap = taps()
    lag = np.arange(BLOCK)[None, :] - np.arange(BLOCK)[:, None] - 1
    toeplitz = np.where(lag >= 0, -tap[np.maximum(lag, 0)], tap[0] * 0).astype(tap.dtype)
    toeplitz += np.eye(BLOCK, dtype=tap.dtype)
    tail = np.broadcast_to(tap[::-1, None], (BLOCK, LANES))
    step = powers(np.arange(BLOCK))[None, :].astype(np.float32)
    return jnp.asarray(np.concatenate([toeplitz, tail], axis=1)), jnp.asarray(step)


VMEM = pl.BlockSpec(memory_space=pltpu.VMEM)
HBM = pl.BlockSpec(memory_space=pltpu.HBM)
LIMIT = pltpu.CompilerParams(vmem_limit_bytes=20 * 1024 * 1024)


def call_closing(rows, shards, traffic, weights):
    series, width = traffic.shape
    return pl.pallas_call(
        functools.partial(closing_kernel, rows),
        in_specs=[HBM, HBM],
        out_specs=[VMEM] * 3,
        out_shape=[
            jax.ShapeDtypeStruct((shards, 1, series), jnp.float32),
            pltpu.VMEM((width // BLOCK - 1, series, LANES), jnp.float32),
            pltpu.VMEM((series, width), jnp.bfloat16),
        ],
        scratch_shapes=[
            pltpu.VMEM((BLOCK, LANES), jnp.bfloat16), pltpu.SemaphoreType.DMA((series // rows + 1,))
        ],
        compiler_params=LIMIT,
        name="closing",
    )(
        pltpu.with_memory_space_constraint(traffic, pltpu.HBM),
        pltpu.with_memory_space_constraint(weights, pltpu.HBM),
    )


def call_residual(shards, pieces, kept, ends, basis, closes, start, weights, step):
    width = kept.shape[1]
    groups = K * width // (pieces * LANES * SUBLANES) + 1
    return pl.pallas_call(
        functools.partial(residual_kernel, shards),
        in_specs=[VMEM] * 7,
        out_specs=VMEM,
        out_shape=jax.ShapeDtypeStruct((pieces, groups, SUBLANES, LANES), jnp.float32),
        scratch_shapes=[pltpu.VMEM((K, width), jnp.float32)],
        compiler_params=LIMIT,
        name="residuals",
    )(kept, ends, basis, closes, start, weights, step)


def call_energy(total, width, every):
    return pl.pallas_call(
        functools.partial(energy_kernel, total),
        in_specs=[VMEM],
        out_specs=[VMEM, VMEM],
        out_shape=[
            jax.ShapeDtypeStruct((K, width), jnp.float32),
            jax.ShapeDtypeStruct((1, width), jnp.float32),
        ],
        name="energies",
    )(pltpu.with_memory_space_constraint(every, pltpu.VMEM))

ROWS = 512

NEAR_FIRST = 11
FAR = (5, 0, 2, 7, 1, 6, 3, 4)
TIME_FIRST = 2


def rotated(items, first):
    items = list(items)
    return items[first:] + items[:first]


def stages(x_size, z_size, cores):
    pairs = z_size // 2

    def device(x, pair, which, core):
        z = 2 * pair + (which if pair < pairs // 2 else 1 - which)
        return (x * z_size + z) * cores + core

    places = [(x, which, core) for x in range(x_size) for which in range(2) for core in range(cores)]
    near = [
        [device(x, pair, which, core) for x, which, core in rotated(places, NEAR_FIRST)]
        for pair in range(pairs)
    ]
    far = [
        [device(x, pair, which, core) for pair in FAR]
        for x, which, core in places
    ]
    return near, far


def exchange(x, axis, groups):
    return lax.all_to_all(x, axis, 0, 0, axis_index_groups=groups, tiled=True)


def shards_fn(shards, total, traffic, start_level, subspace):
    series, width = traffic.shape
    near, far = stages(4, 16, 2)
    pieces = len(near[0])
    weights, step = constants()
    close, ends, kept = call_closing(ROWS, shards, traffic, weights)
    closes = exchange(close, "tm", [rotated(range(shards), TIME_FIRST)])
    part = call_residual(
        shards, pieces, kept, ends, subspace.T, closes, start_level.reshape(1, series), weights, step
    )
    mine = jnp.sum(exchange(part, "prefix", near), axis=0)
    mine = jnp.broadcast_to(mine[None], (len(far[0]),) + mine.shape)
    mine = jnp.sum(exchange(mine, "prefix", far), axis=0)
    every = exchange(jnp.broadcast_to(mine[None], (pieces,) + mine.shape), "prefix", near)
    scores, energy = call_energy(total, width, every)
    return scores, energy.reshape(width)


def solution(mesh):
    def program(traffic, start_level, subspace):
        return jax.shard_map(
            functools.partial(shards_fn, mesh.shape["tm"], traffic.shape[0]),
            mesh=mesh,
            in_specs=(P("prefix", "tm"), P("prefix"), P("prefix", None)),
            out_specs=(P(None, "tm"), P("tm")),
            check_vma=False,
        )(traffic, start_level, subspace)

    return program
```

```python
import functools

import jax
import jax.numpy as jnp
import ml_dtypes
import numpy as np
from jax import lax
from jax.experimental import pallas as pl
from jax.experimental.pallas import tpu as pltpu
from jax.sharding import PartitionSpec as P

BLOCK = 256
LANES = 128
SUBLANES = 4
K = 64
ewma_rate = 0.002


def powers(exponents):
    return (1.0 - ewma_rate) ** np.asarray(exponents, np.float64)


def taps():
    return (ewma_rate * powers(np.arange(BLOCK))).astype(ml_dtypes.bfloat16)


def closing_kernel(rows, x_hbm, weights_hbm, close_ref, ends_ref, x_ref, tail_ref, sems):
    series, width = x_ref.shape
    blocks = width // BLOCK
    steps = series // rows
    ready = pltpu.make_async_copy(weights_hbm.at[:, BLOCK:], tail_ref, sems.at[steps])
    ready.start()
    copies = []
    for i in range(steps):
        at = slice(i * rows, (i + 1) * rows)
        copies.append(pltpu.make_async_copy(x_hbm.at[at], x_ref.at[at], sems.at[i]))
        copies[-1].start()
    block_keep = jnp.float32(powers(BLOCK))
    tile = (LANES, LANES)
    diagonal = lax.broadcasted_iota(jnp.int32, tile, 0) == lax.broadcasted_iota(jnp.int32, tile, 1)
    ready.wait()
    tail = tail_ref[...]
    for i in range(steps):
        at = slice(i * rows, (i + 1) * rows)
        copies[i].wait()
        level = None
        for b in range(blocks):
            end = jnp.dot(
                x_ref[at, b * BLOCK : (b + 1) * BLOCK], tail, preferred_element_type=jnp.float32
            )
            level = end if level is None else end + block_keep * level
            if b + 1 < blocks:
                ends_ref[b, at] = level
        for first in range(0, rows, LANES):
            line = jnp.sum(jnp.where(diagonal, level[first : first + LANES], 0.0), axis=0, keepdims=True)
            close_ref[:, :, i * rows + first : i * rows + first + LANES] = jnp.broadcast_to(
                line[None], (close_ref.shape[0], 1, LANES)
            )


def residual_kernel(
    shards, x_ref, ends_ref, ut_ref, closes_ref, start_ref, weights_ref, step_ref, out_ref, scores_ref
):
    series, width = x_ref.shape
    place = lax.axis_index("tm")

    def weight(table):
        value = jnp.float32(table[0])
        for p in range(1, shards):
            value = jnp.where(place == p, jnp.float32(table[p]), value)
        return value

    line = start_ref[...] * weight([powers(width * p) for p in range(shards)])
    for s in range(shards - 1):
        line += closes_ref[(s - TIME_FIRST) % shards] * weight(
            [powers(width * (p - 1 - s)) if s < p else 0.0 for p in range(shards)]
        )
    basis = ut_ref[...]
    gram = lax.dot_general(basis, basis, (((1,), (1,)), ((), ())), preferred_element_type=jnp.float32)
    entry = jnp.transpose(jnp.broadcast_to(line, (LANES, series)))
    step = step_ref[...]
    squares = []
    residuals = []
    for b in range(width // BLOCK):
        cols = slice(b * BLOCK, (b + 1) * BLOCK)
        local = jnp.dot(x_ref[:, cols], weights_ref[:, :BLOCK], preferred_element_type=jnp.float32)
        level = entry if b == 0 else ends_ref[b - 1] + jnp.float32(powers(b * BLOCK)) * entry
        level = jnp.concatenate([level] * (BLOCK // LANES), axis=1)
        residual = (local - level * step).astype(jnp.bfloat16)
        exact = residual.astype(jnp.float32)
        squares.append(jnp.sum(exact * exact, axis=0, keepdims=True))
        residuals.append(residual)
    for b in range(width // BLOCK):
        scores_ref[:, b * BLOCK : (b + 1) * BLOCK] = jnp.dot(
            basis, residuals[b], preferred_element_type=jnp.float32
        )
    square = jnp.concatenate(squares, axis=1)
    pieces, groups = out_ref.shape[:2]
    halves = pieces * LANES // width
    high = K // halves
    per = K // pieces
    for p in range(pieces):
        j, h = divmod(p, halves)
        cols = slice(j * LANES, (j + 1) * LANES)
        for q in range(groups - 1):
            first = h * high + q * SUBLANES
            out_ref[p, q] = scores_ref[first : first + SUBLANES, cols]
        mine = gram[p * per : (p + 1) * per]
        out_ref[p, groups - 1] = jnp.concatenate(
            [
                square[:, cols],
                jnp.concatenate([mine[: per // 2], mine[per // 2 :]], axis=1),
                jnp.zeros((1, LANES), jnp.float32),
            ],
            axis=0,
        )


def energy_kernel(series, in_ref, scores_ref, energy_ref):
    pieces, groups = in_ref.shape[:2]
    width = scores_ref.shape[1]
    halves = pieces * LANES // width
    high = K // halves
    per = K // pieces
    rows = []
    for p in range(pieces):
        packed = in_ref[p, groups - 1, 1 : 1 + per // 2]
        rows += [packed[:, :K], packed[:, K:]]
    gram = jnp.concatenate(rows, axis=0)
    top = gram.astype(jnp.bfloat16)
    rest = gram - top.astype(jnp.float32)
    middle = rest.astype(jnp.bfloat16)
    low = (rest - middle.astype(jnp.float32)).astype(jnp.bfloat16)
    for p in range(pieces):
        j, h = divmod(p, halves)
        cols = slice(j * LANES, (j + 1) * LANES)
        for q in range(groups - 1):
            first = h * high + q * SUBLANES
            scores_ref[first : first + SUBLANES, cols] = in_ref[p, q]
        if h == 0:
            energy_ref[:, cols] = in_ref[p, groups - 1, 0:1]
    scores = scores_ref[...]
    scores_low = scores.astype(jnp.bfloat16)
    spread = jnp.dot(
        jnp.concatenate([top, middle, low], axis=0), scores_low, preferred_element_type=jnp.float32
    )
    spread = spread[0:K] + spread[K : 2 * K] + spread[2 * K :]
    inside = jnp.sum(scores_low.astype(jnp.float32) * (2.0 * scores - spread), axis=0, keepdims=True)
    energy_ref[...] = (energy_ref[...] - inside) * jnp.float32(1.0 / series)


def constants():
    tap = taps()
    lag = np.arange(BLOCK)[None, :] - np.arange(BLOCK)[:, None] - 1
    toeplitz = np.where(lag >= 0, -tap[np.maximum(lag, 0)], tap[0] * 0).astype(tap.dtype)
    toeplitz += np.eye(BLOCK, dtype=tap.dtype)
    tail = np.broadcast_to(tap[::-1, None], (BLOCK, LANES))
    step = powers(np.arange(BLOCK))[None, :].astype(np.float32)
    return jnp.asarray(np.concatenate([toeplitz, tail], axis=1)), jnp.asarray(step)


VMEM = pl.BlockSpec(memory_space=pltpu.VMEM)
HBM = pl.BlockSpec(memory_space=pltpu.HBM)
LIMIT = pltpu.CompilerParams(vmem_limit_bytes=20 * 1024 * 1024)


def call_closing(rows, shards, traffic, weights):
    series, width = traffic.shape
    return pl.pallas_call(
        functools.partial(closing_kernel, rows),
        in_specs=[HBM, HBM],
        out_specs=[VMEM] * 3,
        out_shape=[
            jax.ShapeDtypeStruct((shards, 1, series), jnp.float32),
            pltpu.VMEM((width // BLOCK - 1, series, LANES), jnp.float32),
            pltpu.VMEM((series, width), jnp.bfloat16),
        ],
        scratch_shapes=[
            pltpu.VMEM((BLOCK, LANES), jnp.bfloat16), pltpu.SemaphoreType.DMA((series // rows + 1,))
        ],
        compiler_params=LIMIT,
        name="closing",
    )(
        pltpu.with_memory_space_constraint(traffic, pltpu.HBM),
        pltpu.with_memory_space_constraint(weights, pltpu.HBM),
    )


def call_residual(shards, pieces, kept, ends, basis, closes, start, weights, step):
    width = kept.shape[1]
    groups = K * width // (pieces * LANES * SUBLANES) + 1
    return pl.pallas_call(
        functools.partial(residual_kernel, shards),
        in_specs=[VMEM] * 7,
        out_specs=VMEM,
        out_shape=jax.ShapeDtypeStruct((pieces, groups, SUBLANES, LANES), jnp.float32),
        scratch_shapes=[pltpu.VMEM((K, width), jnp.float32)],
        compiler_params=LIMIT,
        name="residuals",
    )(kept, ends, basis, closes, start, weights, step)


def call_energy(total, width, every):
    return pl.pallas_call(
        functools.partial(energy_kernel, total),
        in_specs=[VMEM],
        out_specs=[VMEM, VMEM],
        out_shape=[
            jax.ShapeDtypeStruct((K, width), jnp.float32),
            jax.ShapeDtypeStruct((1, width), jnp.float32),
        ],
        name="energies",
    )(pltpu.with_memory_space_constraint(every, pltpu.VMEM))

ROWS = 512

NEAR = (11, 9, 10, 8, 3, 1, 2, 0, 7, 5, 6, 4, 15, 13, 14, 12)
FAR = (5, 0, 2, 1, 7, 6, 3, 4)
TIME_FIRST = 2


def rotated(items, first):
    items = list(items)
    return items[first:] + items[:first]


def stages(x_size, z_size, cores):
    pairs = z_size // 2

    def device(x, pair, which, core):
        z = 2 * pair + (which if pair < pairs // 2 else 1 - which)
        return (x * z_size + z) * cores + core

    places = [(x, which, core) for x in range(x_size) for which in range(2) for core in range(cores)]
    near = [
        [device(x, pair, which, core) for x, which, core in [places[i] for i in NEAR]]
        for pair in range(pairs)
    ]
    far = [
        [device(x, pair, which, core) for pair in FAR]
        for x, which, core in places
    ]
    return near, far


def exchange(x, axis, groups):
    return lax.all_to_all(x, axis, 0, 0, axis_index_groups=groups, tiled=True)


def shards_fn(shards, total, traffic, start_level, subspace):
    series, width = traffic.shape
    near, far = stages(4, 16, 2)
    pieces = len(near[0])
    weights, step = constants()
    close, ends, kept = call_closing(ROWS, shards, traffic, weights)
    closes = exchange(close, "tm", [rotated(range(shards), TIME_FIRST)])
    part = call_residual(
        shards, pieces, kept, ends, subspace.T, closes, start_level.reshape(1, series), weights, step
    )
    mine = jnp.sum(exchange(part, "prefix", near), axis=0)
    mine = jnp.broadcast_to(mine[None], (len(far[0]),) + mine.shape)
    mine = jnp.sum(exchange(mine, "prefix", far), axis=0)
    every = exchange(jnp.broadcast_to(mine[None], (pieces,) + mine.shape), "prefix", near)
    scores, energy = call_energy(total, width, every)
    return scores, energy.reshape(width)


def solution(mesh):
    def program(traffic, start_level, subspace):
        return jax.shard_map(
            functools.partial(shards_fn, mesh.shape["tm"], traffic.shape[0]),
            mesh=mesh,
            in_specs=(P("prefix", "tm"), P("prefix"), P("prefix", None)),
            out_specs=(P(None, "tm"), P("tm")),
            check_vma=False,
        )(traffic, start_level, subspace)

    return program
```

```python
import functools

import jax
import jax.numpy as jnp
import ml_dtypes
import numpy as np
from jax import lax
from jax.experimental import pallas as pl
from jax.experimental.pallas import tpu as pltpu
from jax.sharding import PartitionSpec as P

BLOCK = 256
LANES = 128
SUBLANES = 4
K = 64
ewma_rate = 0.002


def powers(exponents):
    return (1.0 - ewma_rate) ** np.asarray(exponents, np.float64)


def taps():
    return (ewma_rate * powers(np.arange(BLOCK))).astype(ml_dtypes.bfloat16)


def closing_kernel(rows, x_hbm, weights_hbm, close_ref, ends_ref, x_ref, tail_ref, sems):
    series, width = x_ref.shape
    blocks = width // BLOCK
    steps = series // rows
    ready = pltpu.make_async_copy(weights_hbm.at[:, BLOCK:], tail_ref, sems.at[steps])
    ready.start()
    copies = []
    for i in range(steps):
        at = slice(i * rows, (i + 1) * rows)
        copies.append(pltpu.make_async_copy(x_hbm.at[at], x_ref.at[at], sems.at[i]))
        copies[-1].start()
    block_keep = jnp.float32(powers(BLOCK))
    tile = (LANES, LANES)
    diagonal = lax.broadcasted_iota(jnp.int32, tile, 0) == lax.broadcasted_iota(jnp.int32, tile, 1)
    ready.wait()
    tail = tail_ref[...]
    for i in range(steps):
        at = slice(i * rows, (i + 1) * rows)
        copies[i].wait()
        level = None
        for b in range(blocks):
            end = jnp.dot(
                x_ref[at, b * BLOCK : (b + 1) * BLOCK], tail, preferred_element_type=jnp.float32
            )
            level = end if level is None else end + block_keep * level
            if b + 1 < blocks:
                ends_ref[b, at] = level
        for first in range(0, rows, LANES):
            line = jnp.sum(jnp.where(diagonal, level[first : first + LANES], 0.0), axis=0, keepdims=True)
            close_ref[:, :, i * rows + first : i * rows + first + LANES] = jnp.broadcast_to(
                line[None], (close_ref.shape[0], 1, LANES)
            )


def residual_kernel(
    shards, x_ref, ends_ref, ut_ref, closes_ref, start_ref, weights_ref, step_ref, out_ref, scores_ref
):
    series, width = x_ref.shape
    place = lax.axis_index("tm")

    def weight(table):
        value = jnp.float32(table[0])
        for p in range(1, shards):
            value = jnp.where(place == p, jnp.float32(table[p]), value)
        return value

    line = start_ref[...] * weight([powers(width * p) for p in range(shards)])
    for s in range(shards - 1):
        line += closes_ref[TIME.index(s)] * weight(
            [powers(width * (p - 1 - s)) if s < p else 0.0 for p in range(shards)]
        )
    basis = ut_ref[...]
    gram = lax.dot_general(basis, basis, (((1,), (1,)), ((), ())), preferred_element_type=jnp.float32)
    entry = jnp.transpose(jnp.broadcast_to(line, (LANES, series)))
    step = step_ref[...]
    squares = []
    residuals = []
    for b in range(width // BLOCK):
        cols = slice(b * BLOCK, (b + 1) * BLOCK)
        local = jnp.dot(x_ref[:, cols], weights_ref[:, :BLOCK], preferred_element_type=jnp.float32)
        level = entry if b == 0 else ends_ref[b - 1] + jnp.float32(powers(b * BLOCK)) * entry
        level = jnp.concatenate([level] * (BLOCK // LANES), axis=1)
        residual = (local - level * step).astype(jnp.bfloat16)
        exact = residual.astype(jnp.float32)
        squares.append(jnp.sum(exact * exact, axis=0, keepdims=True))
        residuals.append(residual)
    for b in range(width // BLOCK):
        scores_ref[:, b * BLOCK : (b + 1) * BLOCK] = jnp.dot(
            basis, residuals[b], preferred_element_type=jnp.float32
        )
    square = jnp.concatenate(squares, axis=1)
    pieces, groups = out_ref.shape[:2]
    halves = pieces * LANES // width
    high = K // halves
    per = K // pieces
    for p in range(pieces):
        j, h = divmod(p, halves)
        cols = slice(j * LANES, (j + 1) * LANES)
        for q in range(groups - 1):
            first = h * high + q * SUBLANES
            out_ref[p, q] = scores_ref[first : first + SUBLANES, cols]
        mine = gram[p * per : (p + 1) * per]
        out_ref[p, groups - 1] = jnp.concatenate(
            [
                square[:, cols],
                jnp.concatenate([mine[: per // 2], mine[per // 2 :]], axis=1),
                jnp.zeros((1, LANES), jnp.float32),
            ],
            axis=0,
        )


def energy_kernel(series, in_ref, scores_ref, energy_ref):
    pieces, groups = in_ref.shape[:2]
    width = scores_ref.shape[1]
    halves = pieces * LANES // width
    high = K // halves
    per = K // pieces
    rows = []
    for p in range(pieces):
        packed = in_ref[p, groups - 1, 1 : 1 + per // 2]
        rows += [packed[:, :K], packed[:, K:]]
    gram = jnp.concatenate(rows, axis=0)
    top = gram.astype(jnp.bfloat16)
    rest = gram - top.astype(jnp.float32)
    middle = rest.astype(jnp.bfloat16)
    low = (rest - middle.astype(jnp.float32)).astype(jnp.bfloat16)
    for p in range(pieces):
        j, h = divmod(p, halves)
        cols = slice(j * LANES, (j + 1) * LANES)
        for q in range(groups - 1):
            first = h * high + q * SUBLANES
            scores_ref[first : first + SUBLANES, cols] = in_ref[p, q]
        if h == 0:
            energy_ref[:, cols] = in_ref[p, groups - 1, 0:1]
    scores = scores_ref[...]
    scores_low = scores.astype(jnp.bfloat16)
    spread = jnp.dot(
        jnp.concatenate([top, middle, low], axis=0), scores_low, preferred_element_type=jnp.float32
    )
    spread = spread[0:K] + spread[K : 2 * K] + spread[2 * K :]
    inside = jnp.sum(scores_low.astype(jnp.float32) * (2.0 * scores - spread), axis=0, keepdims=True)
    energy_ref[...] = (energy_ref[...] - inside) * jnp.float32(1.0 / series)


def constants():
    tap = taps()
    lag = np.arange(BLOCK)[None, :] - np.arange(BLOCK)[:, None] - 1
    toeplitz = np.where(lag >= 0, -tap[np.maximum(lag, 0)], tap[0] * 0).astype(tap.dtype)
    toeplitz += np.eye(BLOCK, dtype=tap.dtype)
    tail = np.broadcast_to(tap[::-1, None], (BLOCK, LANES))
    step = powers(np.arange(BLOCK))[None, :].astype(np.float32)
    return jnp.asarray(np.concatenate([toeplitz, tail], axis=1)), jnp.asarray(step)


VMEM = pl.BlockSpec(memory_space=pltpu.VMEM)
HBM = pl.BlockSpec(memory_space=pltpu.HBM)
LIMIT = pltpu.CompilerParams(vmem_limit_bytes=20 * 1024 * 1024)


def call_closing(rows, shards, traffic, weights):
    series, width = traffic.shape
    return pl.pallas_call(
        functools.partial(closing_kernel, rows),
        in_specs=[HBM, HBM],
        out_specs=[VMEM] * 3,
        out_shape=[
            jax.ShapeDtypeStruct((shards, 1, series), jnp.float32),
            pltpu.VMEM((width // BLOCK - 1, series, LANES), jnp.float32),
            pltpu.VMEM((series, width), jnp.bfloat16),
        ],
        scratch_shapes=[
            pltpu.VMEM((BLOCK, LANES), jnp.bfloat16), pltpu.SemaphoreType.DMA((series // rows + 1,))
        ],
        compiler_params=LIMIT,
        name="closing",
    )(
        pltpu.with_memory_space_constraint(traffic, pltpu.HBM),
        pltpu.with_memory_space_constraint(weights, pltpu.HBM),
    )


def call_residual(shards, pieces, kept, ends, basis, closes, start, weights, step):
    width = kept.shape[1]
    groups = K * width // (pieces * LANES * SUBLANES) + 1
    return pl.pallas_call(
        functools.partial(residual_kernel, shards),
        in_specs=[VMEM] * 7,
        out_specs=VMEM,
        out_shape=jax.ShapeDtypeStruct((pieces, groups, SUBLANES, LANES), jnp.float32),
        scratch_shapes=[pltpu.VMEM((K, width), jnp.float32)],
        compiler_params=LIMIT,
        name="residuals",
    )(kept, ends, basis, closes, start, weights, step)


def call_energy(total, width, every):
    return pl.pallas_call(
        functools.partial(energy_kernel, total),
        in_specs=[VMEM],
        out_specs=[VMEM, VMEM],
        out_shape=[
            jax.ShapeDtypeStruct((K, width), jnp.float32),
            jax.ShapeDtypeStruct((1, width), jnp.float32),
        ],
        name="energies",
    )(pltpu.with_memory_space_constraint(every, pltpu.VMEM))

ROWS = 512

NEAR = (11, 9, 8, 10, 3, 1, 0, 2, 7, 5, 4, 6, 15, 13, 12, 14)
FAR = (5, 0, 2, 1, 7, 6, 3, 4)
TIME = (2, 0, 3, 1)


def stages(x_size, z_size, cores):
    pairs = z_size // 2

    def device(x, pair, which, core):
        z = 2 * pair + (which if pair < pairs // 2 else 1 - which)
        return (x * z_size + z) * cores + core

    places = [(x, which, core) for x in range(x_size) for which in range(2) for core in range(cores)]
    near = [
        [device(x, pair, which, core) for x, which, core in [places[i] for i in NEAR]]
        for pair in range(pairs)
    ]
    far = [
        [device(x, pair, which, core) for pair in FAR]
        for x, which, core in places
    ]
    return near, far


def exchange(x, axis, groups):
    return lax.all_to_all(x, axis, 0, 0, axis_index_groups=groups, tiled=True)


def shards_fn(shards, total, traffic, start_level, subspace):
    series, width = traffic.shape
    near, far = stages(4, 16, 2)
    pieces = len(near[0])
    weights, step = constants()
    close, ends, kept = call_closing(ROWS, shards, traffic, weights)
    closes = exchange(close, "tm", [list(TIME)])
    part = call_residual(
        shards, pieces, kept, ends, subspace.T, closes, start_level.reshape(1, series), weights, step
    )
    mine = jnp.sum(exchange(part, "prefix", near), axis=0)
    mine = jnp.broadcast_to(mine[None], (len(far[0]),) + mine.shape)
    mine = jnp.sum(exchange(mine, "prefix", far), axis=0)
    every = exchange(jnp.broadcast_to(mine[None], (pieces,) + mine.shape), "prefix", near)
    scores, energy = call_energy(total, width, every)
    return scores, energy.reshape(width)


def solution(mesh):
    def program(traffic, start_level, subspace):
        return jax.shard_map(
            functools.partial(shards_fn, mesh.shape["tm"], traffic.shape[0]),
            mesh=mesh,
            in_specs=(P("prefix", "tm"), P("prefix"), P("prefix", None)),
            out_specs=(P(None, "tm"), P("tm")),
            check_vma=False,
        )(traffic, start_level, subspace)

    return program
```
